32 devices in a mesh: dp: 2 (over y), expert: 16 (over z, x, core).
Axes of the slice: x: 2, y: 2, z: 4, core: 2. Of those that a mesh axis runs over, the one named last changes fastest.
Arguments:
- tokens: bfloat16 [512, 2880], P(('dp', 'expert')), may hold values from -6 to 6
- grad_out: bfloat16 [512, 2880], P(('dp', 'expert')), may hold values from -6 to 6
- route_ids: int32 [512, 4], P(('dp', 'expert')), may hold values from 0 to 4, all different within a row; in each aligned block of 16 rows (0 to 15, 16 to 31, ...) at most 16 rows name the same one
- route_prob: float32 [512, 4], P(('dp', 'expert')), may hold values from 0.05 to 1
- device_expert: int32 [16], replicated, may hold values from 0 to 4, as said below
- unit_count: int32 [16], replicated, may hold values from 264 to 480, as said below
- expert_weights: bfloat16 [16, 480, 8640], P('expert'), may hold values from -0.109375 to 0.109375
Outputs:
- grad_tokens: bfloat16 [512, 2880], P(('dp', 'expert'))
- grad_weights: bfloat16 [16, 480, 8640], P('expert', 'dp')
The draws below stay inside these ranges and needn't reach their ends.
Inputs may be any that keep to these rules, and one draw needn't show every extreme that they name: `route_ids`: each row names 4 different experts; the 16 rows of one device name each expert at most 16 times, and in every draw some device names some expert exactly 16 times. `device_expert`: aligned blocks of 16 indices of expert hold 5 experts, ids rising by one from 5 times the block's number; the indices of one expert are consecutive, 3 or 4 of them; every expert has a group. `unit_count`: the counts of the indices of one expert sum to 1440; rows of expert_weights at or past a slot's count are not part of the model.
All inputs are finite; a program needn't handle non-finite values.
Results may differ from the reference program's by a relative error of at most 0.0058.
Values may be sent and summed in bfloat16 or wider, within the bound.
A program may use at most 128 MiB of HBM per device.

```python
import math
import jax
import jax.numpy as jnp
import numpy as np
from jax import lax

D = 2880
HID = 1440
TOPK = 4
TOK_DEV = 16
SLOT = 480
EXPERTS = 5
CAP = 16
TOKENS = 512
N_DP = 2
N_EXPERT = 16


def plan_tables(key):
    blocks = N_EXPERT // 16
    larger = jax.random.randint(jax.random.fold_in(key, 11), (blocks,), 0, 5)
    group_sizes = 3 + (jnp.arange(5)[None, :] == larger[:, None]).astype(jnp.int32)
    group_ends = jnp.cumsum(group_sizes, axis=1)
    position = jnp.arange(16)
    local_id = jnp.sum((position[None, :, None] >= group_ends[:, None, :]).astype(jnp.int32), axis=2)
    experts = local_id + 5 * jnp.arange(blocks)[:, None]
    group_begin = jnp.take_along_axis(group_ends - group_sizes, local_id, axis=1)
    member = position[None, :] - group_begin
    group_size = jnp.take_along_axis(group_sizes, local_id, axis=1)
    unit_step = HID // 60
    shifts = jax.random.randint(jax.random.fold_in(key, 12), (blocks, 2), -4, 5) * unit_step
    shifts = shifts.at[0, 0].set(4 * unit_step)
    base_units = HID // 4
    parity_sign = 1 - 2 * (member % 2)
    pair_id = jnp.minimum(member // 2, 1)
    four_counts = base_units + parity_sign * jnp.take_along_axis(shifts, pair_id, axis=1)
    counts = jnp.where(group_size == 4, four_counts, HID // 3)
    return (experts.reshape(-1).astype(jnp.int32), counts.reshape(-1).astype(jnp.int32))


def draw_device_expert(key, part):
    return plan_tables(key)[0]


def draw_unit_count(key, part):
    return plan_tables(key)[1]


def block_levels(own_key, shape, pieces, low, largest):
    def one(axis_at, shards_of):
        draws = jax.random.uniform(jax.random.fold_in(jax.random.fold_in(own_key, 6), axis_at), (shards_of,), jnp.float32, low / len(pieces), largest / len(pieces))
        return jnp.repeat(jnp.exp(draws), shape[axis_at] // shards_of).reshape((-1,) + (1,) * (len(shape) - axis_at - 1))

    loudness = one(*pieces[0])
    for cut in pieces[1:]:
        loudness = loudness * one(*cut)
    return loudness


def routed_block(rng, own, number, rows, amount, top, limit, lean):
    order = jax.random.permutation(rng, amount)
    heavy_load, common = portions_of(amount, rows * top, limit, lean, True), portions_of(amount, rows * top, limit, lean, False)
    places = jnp.arange(amount)

    def named(tallies, rotation):
        used = int((tallies > 0).sum())
        fixed = max(1, used // 4)
        shifted = fixed + (places - fixed + rotation * (used - fixed)) % max(1, amount - fixed)
        return jnp.zeros((amount,), jnp.int32).at[order[jnp.where(places < fixed, places, shifted)]].set(jnp.asarray(tallies, jnp.int32))

    tallies = jnp.where(number % 4 == 0, named(heavy_load, number // 4), named(common, number - number // 4 - 1))
    mixed = jax.random.permutation(jax.random.fold_in(own, 3), amount)
    donor, taker = mixed[0:amount // 2 * 2:2], mixed[1:amount // 2 * 2:2]
    margin = jnp.minimum(tallies[donor] - 1, limit - tallies[taker]) // 2
    margin = jnp.where((donor == order[0]) | (taker == order[0]) | (tallies[taker] == 0), 0, jnp.maximum(margin, 0))
    shifted = jax.random.randint(jax.random.fold_in(own, 4), (amount // 2,), 0, 1 << 20) % (margin + 1)
    tallies = tallies.at[donor].add(-shifted).at[taker].add(shifted)
    labels = jnp.searchsorted(jnp.cumsum(tallies), jnp.arange(rows * top), side="right").astype(jnp.int32)
    grid = labels.reshape(top, rows).T
    grid = grid[jax.random.permutation(jax.random.fold_in(own, 1), rows)]
    rotation = jax.random.randint(jax.random.fold_in(own, 2), (rows, 1), 0, top)
    return jnp.take_along_axis(grid, (jnp.arange(top)[None, :] + rotation) % top, axis=1)


def portions_of(amount, total, most, skew, full):
    weights = [(1 << 20) // math.isqrt(rank ** skew) + 1 for rank in range(1, amount + 1)]
    largest = most if full else min(most, max(-(-total // amount), total * weights[0] // sum(weights)))
    least = 1 if total - largest >= amount - 1 else 0
    given, rest = [largest] + [least] * (amount - 1), total - largest - least * (amount - 1)
    while rest > 0:
        movable = [i for i in range(1, amount) if given[i] < largest] or [i for i in range(1, amount) if given[i] < most]
        whole, budget = sum([weights[i] for i in movable]), rest
        for i in movable:
            addition = min(most - given[i], max(1, budget * weights[i] // whole), rest)
            given[i] = given[i] + addition
            rest = rest - addition
    return np.array(given)


def bell_draw(rng, extent, deviation, bound, pieces=(), kind=jnp.bfloat16):
    values = deviation * jax.random.normal(rng, extent, jnp.float32)
    if pieces:
        values = values * block_levels(rng, extent, pieces, -0.22, 0.18)
    return jnp.clip(values, -bound, bound).astype(kind)


def setup_inputs(seed: int = 0) -> dict:
    keys = jax.random.split(jax.random.key(seed), 8)
    tokens = bell_draw(keys[0], (TOKENS, D), 1.0, 6.0, ((0, 32),))
    grad_out = bell_draw(keys[1], (TOKENS, D), 1.0, 6.0, ((0, 32),))
    route_ids_keys = jax.random.split(jax.random.fold_in(keys[2], 1), TOKENS // TOK_DEV)
    route_ids_turns = jax.random.permutation(jax.random.fold_in(keys[2], 3), TOKENS // TOK_DEV)
    route_ids = jax.vmap(lambda own, number: routed_block(jax.random.fold_in(keys[2], 2), own, number, TOK_DEV, EXPERTS, TOPK, CAP, 1))(route_ids_keys, route_ids_turns).reshape((TOKENS, TOPK))
    route_prob = jnp.clip(jnp.exp(math.log(1.0) - 2.9957323 * jax.random.uniform(keys[3], (TOKENS, TOPK), jnp.float32) ** block_levels(keys[3], (TOKENS, TOPK), ((0, 32),), -0.2, 0.2)), 0.05, 1.0)
    device_expert = draw_device_expert(jax.random.fold_in(keys[7], 71), 0)
    unit_count = draw_unit_count(jax.random.fold_in(keys[7], 71), 0)
    expert_weights = bell_draw(keys[6], (N_EXPERT, SLOT, 3 * D), D ** -0.5, 0.109375, ((0, 16),))
    return dict(tokens=tokens, grad_out=grad_out, route_ids=route_ids, route_prob=route_prob, device_expert=device_expert, unit_count=unit_count, expert_weights=expert_weights)


def silu_parts(preact):
    sigma = jax.nn.sigmoid(preact)
    return preact * sigma, sigma * (1.0 + preact * (1.0 - sigma))


def route_table(ids_block, prob_block):
    flat_ids = ids_block.reshape(-1)
    onehot = (flat_ids[:, None] == jnp.arange(EXPERTS, dtype=jnp.int32)[None, :]).astype(jnp.int32)
    rank_of = jnp.sum(onehot * jnp.cumsum(onehot, axis=0), axis=1) - 1
    matched = (flat_ids[None, None, :] == jnp.arange(EXPERTS, dtype=jnp.int32)[:, None, None]) & (rank_of[None, None, :] == jnp.arange(CAP, dtype=jnp.int32)[None, :, None])
    owner = jnp.arange(flat_ids.shape[0], dtype=jnp.int32) // TOPK
    token_ids = jnp.sum(jnp.where(matched, owner[None, None, :], 0), axis=2).astype(jnp.int32)
    route_weight = jnp.sum(jnp.where(matched, prob_block.reshape(-1)[None, None, :], 0.0), axis=2)
    live_slot = jnp.any(matched, axis=2)
    return token_ids, route_weight, live_slot


def reference(tokens, grad_out, route_ids, route_prob, device_expert, unit_count, expert_weights):
    sources = N_DP * N_EXPERT
    token_ids, route_weight, live_slot = jax.vmap(route_table)(route_ids.reshape(sources, TOK_DEV, TOPK), route_prob.reshape(sources, TOK_DEV, TOPK))
    token_ids = token_ids + (jnp.arange(sources, dtype=jnp.int32) * TOK_DEV)[:, None, None]
    contract = (((1,), (1,)), ((), ()))
    rows_first = (((0,), (0,)), ((), ()))

    def one_slot(accum, slot_index):
        expert_id = device_expert[slot_index]
        slot_weights = expert_weights[slot_index]
        row_index = jnp.take(token_ids, expert_id, axis=1).reshape(-1).astype(jnp.int32)
        row_scale = jnp.take(route_weight, expert_id, axis=1).reshape(-1)
        row_live = jnp.take(live_slot, expert_id, axis=1).reshape(-1)
        token_rows = jnp.where(row_live[:, None], tokens[row_index], jnp.zeros((), tokens.dtype))
        grad_rows = jnp.where(row_live[:, None], row_scale[:, None] * grad_out[row_index].astype(jnp.float32), 0.0).astype(jnp.bfloat16)
        gate_rows = slot_weights[:, :D]
        up_rows = slot_weights[:, D:2 * D]
        down_rows = slot_weights[:, 2 * D:]
        gate_pre = lax.dot_general(token_rows, gate_rows, contract, preferred_element_type=jnp.float32)
        up_pre = lax.dot_general(token_rows, up_rows, contract, preferred_element_type=jnp.float32)
        back_grad = lax.dot_general(grad_rows, down_rows, contract, preferred_element_type=jnp.float32)
        unit_mask = (jnp.arange(SLOT, dtype=jnp.int32) < unit_count[slot_index]).astype(jnp.float32)
        active, slope = silu_parts(gate_pre)
        hidden = (active * up_pre * unit_mask).astype(jnp.bfloat16)
        grad_gate = (back_grad * up_pre * slope * unit_mask).astype(jnp.bfloat16)
        grad_up = (back_grad * active * unit_mask).astype(jnp.bfloat16)
        partial_value = jnp.dot(grad_gate, gate_rows, preferred_element_type=jnp.float32) + jnp.dot(grad_up, up_rows, preferred_element_type=jnp.float32)
        accum = accum.at[row_index].add(jnp.where(row_live[:, None], partial_value, 0.0))
        grad_slot = jnp.concatenate([
            lax.dot_general(grad_gate, token_rows, rows_first, preferred_element_type=jnp.float32),
            lax.dot_general(grad_up, token_rows, rows_first, preferred_element_type=jnp.float32),
            lax.dot_general(hidden, grad_rows, rows_first, preferred_element_type=jnp.float32)], axis=1)
        return accum, grad_slot.astype(jnp.bfloat16)

    accum, grad_slots = lax.scan(one_slot, jnp.zeros((TOKENS, D), jnp.float32), jnp.arange(N_EXPERT, dtype=jnp.int32))
    return accum.astype(jnp.bfloat16), grad_slots
```

```python
import jax
import jax.numpy as jnp
from jax import lax
from jax.sharding import PartitionSpec as P

AXES = ("dp", "expert")


def silu_parts(preact):
    sigma = jax.nn.sigmoid(preact)
    return (preact * sigma, sigma * (1.0 + preact * (1.0 - sigma)))


def unit_work(token_rows, grad_rows, slot_weights, unit_mask):
    width = token_rows.shape[1]
    gate_rows = slot_weights[:, :width]
    up_rows = slot_weights[:, width : 2 * width]
    down_rows = slot_weights[:, 2 * width :]
    contract = (((1,), (1,)), ((), ()))
    gate_pre = lax.dot_general(token_rows, gate_rows, contract, preferred_element_type=jnp.float32)
    up_pre = lax.dot_general(token_rows, up_rows, contract, preferred_element_type=jnp.float32)
    back_grad = lax.dot_general(grad_rows, down_rows, contract, preferred_element_type=jnp.float32)
    active, slope = silu_parts(gate_pre)
    hidden = (active * up_pre * unit_mask).astype(jnp.bfloat16)
    grad_gate = (back_grad * up_pre * slope * unit_mask).astype(jnp.bfloat16)
    grad_up = (back_grad * active * unit_mask).astype(jnp.bfloat16)
    partial_value = jnp.dot(grad_gate, gate_rows, preferred_element_type=jnp.float32) + jnp.dot(
        grad_up, up_rows, preferred_element_type=jnp.float32
    )
    return (partial_value, hidden, grad_gate, grad_up)


def weight_terms(token_rows, grad_rows, hidden, grad_gate, grad_up):
    rows_first = (((0,), (0,)), ((), ()))
    return jnp.concatenate(
        [
            lax.dot_general(grad_gate, token_rows, rows_first, preferred_element_type=jnp.float32),
            lax.dot_general(grad_up, token_rows, rows_first, preferred_element_type=jnp.float32),
            lax.dot_general(hidden, grad_rows, rows_first, preferred_element_type=jnp.float32),
        ],
        axis=1,
    )


def send_back(partial_value):
    return lax.all_to_all(partial_value, "expert", split_axis=0, concat_axis=0, tiled=True)


def routed_shards(tokens, grad_out, route_ids, route_prob, device_expert, unit_count, expert_weights):
    token_count, width = tokens.shape
    top_count = route_ids.shape[1]
    devices = lax.axis_size("expert")
    experts = 5 * devices // 16
    capacity = token_count * top_count * 4 // devices
    flat_ids = route_ids.reshape(-1)
    onehot = (flat_ids[:, None] == jnp.arange(experts, dtype=jnp.int32)[None, :]).astype(jnp.int32)
    rank_of = jnp.sum(onehot * jnp.cumsum(onehot, axis=0), axis=1) - 1
    picked = (flat_ids[None, None, :] == device_expert[:, None, None]) & (
        rank_of[None, None, :] == jnp.arange(capacity, dtype=jnp.int32)[None, :, None]
    )
    picked = picked.astype(jnp.float32).reshape(devices * capacity, token_count * top_count)
    by_token = picked.reshape(devices * capacity, token_count, top_count).sum(axis=2)
    route_scale = jnp.dot(picked, route_prob.reshape(-1), precision=lax.Precision.HIGHEST)
    by_token_low = by_token.astype(jnp.bfloat16)
    sent_rows = jnp.dot(by_token_low, tokens, preferred_element_type=jnp.float32).astype(
        jnp.bfloat16
    )
    sent_grads = (
        route_scale[:, None] * jnp.dot(by_token_low, grad_out, preferred_element_type=jnp.float32)
    ).astype(jnp.bfloat16)
    outgoing = jnp.stack([sent_rows, sent_grads], axis=1).reshape(devices, capacity, 2, width)
    position = lax.axis_index("expert")
    unit_limit = lax.dynamic_index_in_dim(unit_count, position, keepdims=False)
    slot_weights = expert_weights[0]
    slot_units = slot_weights.shape[0]
    unit_mask = (jnp.arange(slot_units, dtype=jnp.int32) < unit_limit).astype(jnp.float32)
    arrived = lax.all_to_all(outgoing, "expert", split_axis=0, concat_axis=0, tiled=True)
    row_pairs = arrived.reshape(-1, 2, width)
    partial_value, hidden, grad_gate, grad_up = unit_work(
        row_pairs[:, 0], row_pairs[:, 1], slot_weights, unit_mask
    )
    leading = (arrived.shape[0], arrived.shape[1])
    returned, all_rows, hidden, grad_gate, grad_up = (
        send_back(partial_value.reshape(leading + (width,))),
        arrived,
        hidden.reshape(leading + (slot_units,)),
        grad_gate.reshape(leading + (slot_units,)),
        grad_up.reshape(leading + (slot_units,)),
    )
    row_pairs = all_rows.reshape(-1, 2, width)
    token_rows = row_pairs[:, 0]
    grad_rows = row_pairs[:, 1]
    hidden = hidden.reshape(-1, slot_units)
    grad_gate = grad_gate.reshape(-1, slot_units)
    grad_up = grad_up.reshape(-1, slot_units)
    term_block = weight_terms(token_rows, grad_rows, hidden, grad_gate, grad_up)
    grad_weights = lax.psum_scatter(term_block, "dp", scatter_dimension=0, tiled=True)
    parts = returned.reshape(devices * capacity, width)
    grad_tokens = lax.dot_general(
        by_token,
        parts,
        (((0,), (0,)), ((), ())),
        precision=lax.Precision.HIGHEST,
        preferred_element_type=jnp.float32,
    )
    return (grad_tokens.astype(jnp.bfloat16), grad_weights.astype(jnp.bfloat16)[None])


def dense_shards(tokens, grad_out, route_ids, route_prob, device_expert, unit_count, expert_weights):
    width = tokens.shape[1]
    devices = lax.axis_size("expert")
    experts = 5 * devices // 16
    half = expert_weights.shape[1] // lax.axis_size("dp")
    named = route_ids[:, :, None] == jnp.arange(experts, dtype=jnp.int32)[None, None, :]
    scales = jnp.sum(jnp.where(named, route_prob[:, :, None], 0.0), axis=1)
    x = lax.all_gather(tokens, AXES, axis=0, tiled=True)
    grads = lax.all_gather(grad_out, AXES, axis=0, tiled=True)
    scales = lax.all_gather(scales, AXES, axis=0, tiled=True)
    position = lax.axis_index("expert")
    expert = lax.dynamic_index_in_dim(device_expert, position, keepdims=False)
    limit = lax.dynamic_index_in_dim(unit_count, position, keepdims=False)
    scale = jnp.sum(jnp.where(jnp.arange(experts)[None, :] == expert, scales, 0.0), axis=1)
    dy = (scale[:, None] * grads.astype(jnp.float32)).astype(jnp.bfloat16)
    first = lax.axis_index("dp") * half
    weights = lax.dynamic_slice_in_dim(expert_weights[0], first, half, axis=0)
    mask = (first + jnp.arange(half, dtype=jnp.int32) < limit)[None, :]
    gate, up, down = (weights[:, i * width : (i + 1) * width] for i in range(3))
    contract = (((1,), (1,)), ((), ()))
    rows_first = (((0,), (0,)), ((), ()))
    f32 = jnp.float32
    g = lax.dot_general(x, gate, contract, preferred_element_type=f32)
    v = lax.dot_general(x, up, contract, preferred_element_type=f32)
    b = lax.dot_general(dy, down, contract, preferred_element_type=f32)
    sigma = jax.nn.sigmoid(g)
    active = g * sigma
    slope = sigma * (1.0 + g * (1.0 - sigma))
    hidden = jnp.where(mask, active * v, 0.0).astype(jnp.bfloat16)
    grad_gate = jnp.where(mask, b * v * slope, 0.0).astype(jnp.bfloat16)
    grad_up = jnp.where(mask, b * active, 0.0).astype(jnp.bfloat16)
    partial = jnp.dot(grad_gate, gate, preferred_element_type=f32) + jnp.dot(
        grad_up, up, preferred_element_type=f32
    )
    grad_tokens = lax.psum_scatter(partial, AXES, scatter_dimension=0, tiled=True)
    grad_weights = jnp.concatenate(
        [
            lax.dot_general(a, c, rows_first, preferred_element_type=f32).astype(jnp.bfloat16)
            for a, c in ((grad_gate, x), (grad_up, x), (hidden, dy))
        ],
        axis=1,
    )
    return grad_tokens.astype(jnp.bfloat16), grad_weights[None]


def shards(tokens, grad_out, route_ids, *rest):
    token_count = tokens.shape[0]
    capacity = token_count * route_ids.shape[1] * 4 // lax.axis_size("expert")
    form = dense_shards if capacity >= token_count else routed_shards
    return form(tokens, grad_out, route_ids, *rest)


def solution(mesh):
    in_specs = (P(AXES, None),) * 4 + (P(), P(), P("expert", None, None))
    out_specs = (P(AXES, None), P("expert", "dp", None))
    return jax.shard_map(shards, mesh=mesh, in_specs=in_specs, out_specs=out_specs, check_vma=False)
```

```python
import functools

import jax
import jax.numpy as jnp
from jax import lax
from jax.experimental import pallas as pl
from jax.experimental.pallas import tpu as pltpu
from jax.sharding import PartitionSpec as P

AXES = ("dp", "expert")


def silu_parts(preact):
    sigma = jax.nn.sigmoid(preact)
    return (preact * sigma, sigma * (1.0 + preact * (1.0 - sigma)))


def unit_work(token_rows, grad_rows, slot_weights, unit_mask):
    width = token_rows.shape[1]
    gate_rows = slot_weights[:, :width]
    up_rows = slot_weights[:, width : 2 * width]
    down_rows = slot_weights[:, 2 * width :]
    contract = (((1,), (1,)), ((), ()))
    gate_pre = lax.dot_general(token_rows, gate_rows, contract, preferred_element_type=jnp.float32)
    up_pre = lax.dot_general(token_rows, up_rows, contract, preferred_element_type=jnp.float32)
    back_grad = lax.dot_general(grad_rows, down_rows, contract, preferred_element_type=jnp.float32)
    active, slope = silu_parts(gate_pre)
    hidden = (active * up_pre * unit_mask).astype(jnp.bfloat16)
    grad_gate = (back_grad * up_pre * slope * unit_mask).astype(jnp.bfloat16)
    grad_up = (back_grad * active * unit_mask).astype(jnp.bfloat16)
    partial_value = jnp.dot(grad_gate, gate_rows, preferred_element_type=jnp.float32) + jnp.dot(
        grad_up, up_rows, preferred_element_type=jnp.float32
    )
    return (partial_value, hidden, grad_gate, grad_up)


def weight_terms(token_rows, grad_rows, hidden, grad_gate, grad_up):
    rows_first = (((0,), (0,)), ((), ()))
    return jnp.concatenate(
        [
            lax.dot_general(grad_gate, token_rows, rows_first, preferred_element_type=jnp.float32),
            lax.dot_general(grad_up, token_rows, rows_first, preferred_element_type=jnp.float32),
            lax.dot_general(hidden, grad_rows, rows_first, preferred_element_type=jnp.float32),
        ],
        axis=1,
    )


def send_back(partial_value):
    return lax.all_to_all(partial_value, "expert", split_axis=0, concat_axis=0, tiled=True)


def routed_shards(tokens, grad_out, route_ids, route_prob, device_expert, unit_count, expert_weights):
    token_count, width = tokens.shape
    top_count = route_ids.shape[1]
    devices = lax.axis_size("expert")
    experts = 5 * devices // 16
    capacity = token_count * top_count * 4 // devices
    flat_ids = route_ids.reshape(-1)
    onehot = (flat_ids[:, None] == jnp.arange(experts, dtype=jnp.int32)[None, :]).astype(jnp.int32)
    rank_of = jnp.sum(onehot * jnp.cumsum(onehot, axis=0), axis=1) - 1
    picked = (flat_ids[None, None, :] == device_expert[:, None, None]) & (
        rank_of[None, None, :] == jnp.arange(capacity, dtype=jnp.int32)[None, :, None]
    )
    picked = picked.astype(jnp.float32).reshape(devices * capacity, token_count * top_count)
    by_token = picked.reshape(devices * capacity, token_count, top_count).sum(axis=2)
    route_scale = jnp.dot(picked, route_prob.reshape(-1), precision=lax.Precision.HIGHEST)
    by_token_low = by_token.astype(jnp.bfloat16)
    sent_rows = jnp.dot(by_token_low, tokens, preferred_element_type=jnp.float32).astype(
        jnp.bfloat16
    )
    sent_grads = (
        route_scale[:, None] * jnp.dot(by_token_low, grad_out, preferred_element_type=jnp.float32)
    ).astype(jnp.bfloat16)
    outgoing = jnp.stack([sent_rows, sent_grads], axis=1).reshape(devices, capacity, 2, width)
    position = lax.axis_index("expert")
    unit_limit = lax.dynamic_index_in_dim(unit_count, position, keepdims=False)
    slot_weights = expert_weights[0]
    slot_units = slot_weights.shape[0]
    unit_mask = (jnp.arange(slot_units, dtype=jnp.int32) < unit_limit).astype(jnp.float32)
    arrived = lax.all_to_all(outgoing, "expert", split_axis=0, concat_axis=0, tiled=True)
    row_pairs = arrived.reshape(-1, 2, width)
    partial_value, hidden, grad_gate, grad_up = unit_work(
        row_pairs[:, 0], row_pairs[:, 1], slot_weights, unit_mask
    )
    leading = (arrived.shape[0], arrived.shape[1])
    returned, all_rows, hidden, grad_gate, grad_up = (
        send_back(partial_value.reshape(leading + (width,))),
        arrived,
        hidden.reshape(leading + (slot_units,)),
        grad_gate.reshape(leading + (slot_units,)),
        grad_up.reshape(leading + (slot_units,)),
    )
    row_pairs = all_rows.reshape(-1, 2, width)
    token_rows = row_pairs[:, 0]
    grad_rows = row_pairs[:, 1]
    hidden = hidden.reshape(-1, slot_units)
    grad_gate = grad_gate.reshape(-1, slot_units)
    grad_up = grad_up.reshape(-1, slot_units)
    term_block = weight_terms(token_rows, grad_rows, hidden, grad_gate, grad_up)
    grad_weights = lax.psum_scatter(term_block, "dp", scatter_dimension=0, tiled=True)
    parts = returned.reshape(devices * capacity, width)
    grad_tokens = lax.dot_general(
        by_token,
        parts,
        (((0,), (0,)), ((), ())),
        precision=lax.Precision.HIGHEST,
        preferred_element_type=jnp.float32,
    )
    return (grad_tokens.astype(jnp.bfloat16), grad_weights.astype(jnp.bfloat16)[None])


MESH = pl.DeviceIdType.MESH
STEP = 256


def dense_kernel(
    nz, half, tok, width,
    x_in, g_in, w_in, sel_ref, mask_ref, gt_out, gw_out,
    xs, gs, dy, w, wu, gg, gu, hid, acc, send1, recv1, send2a, recv2a, send2b, recv2b,
    send3a, recv3a, send3b, recv3b, send4, recv4, gw, up,
    local_sem, recv_sem, sz, sx, sy, ss, rs_send, rs_recv,
):
    f32, bf16 = jnp.float32, jnp.bfloat16
    y = lax.axis_index("dp")
    position = lax.axis_index("expert")
    z, x, c = position // 4, (position // 2) % 2, position % 2
    oy, ox, oc = 1 - y, 1 - x, 1 - c

    def place(yy, zz, xx, cc):
        return (yy, zz * 4 + xx * 2 + cc)

    def slot(cc, yy, xx, zz):
        return ((cc * 2 + yy) * 2 + xx) * nz + zz

    def rows(s, count=1):
        return pl.ds(pl.multiple_of(s * tok, tok), count * tok)

    zs = [lax.rem(z + k, nz) for k in range(nz)]
    x_nbr, y_nbr, sib = place(y, z, ox, c), place(oy, z, x, c), place(y, z, x, oc)
    z_nbrs = [place(y, zs[k], x, c) for k in range(1, nz)]

    mine = slot(c, y, x, z)
    first = pl.multiple_of(y * half, 16)
    own = [
        pltpu.make_async_copy(x_in, xs.at[rows(mine)], local_sem.at[0]),
        pltpu.make_async_copy(g_in, gs.at[rows(mine)], local_sem.at[1]),
    ]
    load_w = pltpu.make_async_copy(w_in.at[0, pl.ds(first, half)], w, local_sem.at[2])
    for copy in own + [load_w]:
        copy.start()
    barrier = pltpu.get_barrier_semaphore()
    peers = [x_nbr, y_nbr, sib] + z_nbrs
    for peer in peers:
        pl.semaphore_signal(barrier, inc=1, device_id=peer, device_id_type=MESH)
    pl.semaphore_wait(barrier, len(peers))

    bufs = (xs, gs)
    sent = []

    def describe(p, s, target, sem):
        return pltpu.make_async_remote_copy(
            src_ref=bufs[p].at[rows(s)], dst_ref=bufs[p].at[rows(s)],
            send_sem=sem, recv_sem=recv_sem.at[p, s], device_id=target, device_id_type=MESH,
        )

    counts = {}

    def send(p, s, name, target):
        sems = {"x": sx, "y": sy, "s": ss, "z": sz}[name]
        index = counts.get((p, name), 0)
        counts[(p, name)] = index + 1
        copy = describe(p, s, target, sems.at[p, index])
        copy.start()
        sent.append(copy)

    def arrived(p, s):
        describe(p, s, sib, ss.at[p, 0]).wait_recv()

    order = [0, 1, nz - 1] + list(range(2, nz - 1))
    for p in range(2):
        own[p].wait()
        for target in z_nbrs:
            send(p, mine, "z", target)
        send(p, mine, "x", x_nbr)
        send(p, mine, "y", y_nbr)
        send(p, mine, "s", sib)
    for k in order[1:]:
        for p in range(2):
            s = slot(c, y, x, zs[k])
            arrived(p, s)
            send(p, s, "x", x_nbr)
            send(p, s, "y", y_nbr)
            send(p, s, "s", sib)
    for k in order:
        s = slot(c, y, ox, zs[k])
        arrived(0, s)
        send(0, s, "y", y_nbr)
        send(0, s, "s", sib)
        s = slot(c, oy, x, zs[k])
        arrived(1, s)
        send(1, s, "x", x_nbr)
        send(1, s, "s", sib)
    load_w.wait()
    wu[...] = w[:, width : 2 * width]
    for k in order:
        for p, s in ((0, slot(c, oy, x, zs[k])), (1, slot(c, y, ox, zs[k]))):
            arrived(p, s)
            send(p, s, "s", sib)
    for k in order:
        for p in range(2):
            s = slot(c, oy, ox, zs[k])
            arrived(p, s)
            send(p, s, "s", sib)
    for k in range(nz):
        for yy in range(2):
            for xx in range(2):
                for p in range(2):
                    arrived(p, slot(oc, yy, xx, k))
    for copy in sent:
        copy.wait_send()

    contract = (((1,), (1,)), ((), ()))
    block = 4 * nz * tok // 2
    tail = width // 128 * 128

    def forward(i, carry):
        r = pl.ds(pl.multiple_of(i * block, block), block)
        scale = jnp.sum(gs[r, tail:].astype(f32) * sel_ref[...], axis=1, keepdims=True)
        dy[r, :] = (scale * gs[r, :width].astype(f32)).astype(bf16)
        token_rows = xs[r, :]
        g = lax.dot_general(token_rows, w[:, :width], contract, preferred_element_type=f32)
        v = lax.dot_general(token_rows, wu[...], contract, preferred_element_type=f32)
        b = lax.dot_general(dy[r, :], w[:, 2 * width :], contract, preferred_element_type=f32)
        live = jnp.broadcast_to(mask_ref[...], g.shape) > 0.0
        sigma = 1.0 / (1.0 + jnp.exp(-g))
        active = g * sigma
        hid[r, :] = jnp.where(live, active * v, 0.0).astype(bf16)
        gg[r, :] = jnp.where(live, b * v * (sigma * (1.0 + g * (1.0 - sigma))), 0.0).astype(bf16)
        gu[r, :] = jnp.where(live, b * active, 0.0).astype(bf16)
        return carry

    lax.fori_loop(0, 8 * nz * tok // block, forward, 0)

    group = nz * tok
    all_rows = 4 * group
    cut = (width // 128 + 1) // 2 * 128
    half_cols = (pl.ds(0, cut), pl.ds(cut, width - cut))
    spans = [(at, min(STEP, end - at)) for begin, end in ((0, cut), (cut, width)) for at in range(begin, end, STEP)]

    def partial(side, at, size):
        r = pl.ds(pl.multiple_of(side * all_rows, all_rows), all_rows)
        return jnp.dot(gg[r, :], w[:, at : at + size], preferred_element_type=f32) + jnp.dot(
            gu[r, :], wu[:, at : at + size], preferred_element_type=f32
        )

    def exchange(index, src, dst, target):
        return pltpu.make_async_remote_copy(
            src_ref=src, dst_ref=dst, send_sem=rs_send.at[index], recv_sem=rs_recv.at[index],
            device_id=target, device_id_type=MESH,
        )

    core = [exchange(h, send1.at[:, half_cols[h]], recv1.at[:, half_cols[h]], sib) for h in range(2)]
    for at, size in spans:
        send1[:, at : at + size] = partial(oc, at, size).astype(bf16)
        if at + size == cut:
            core[0].start()
    core[1].start()
    for at, size in spans:
        acc[:, at : at + size] = partial(c, at, size)

    def grp(yy, xx, count=1):
        return pl.ds(pl.multiple_of((yy * 2 + xx) * group, group), count * group)

    lo, hi = slice(0, cut), slice(cut, width)
    second = [exchange(2, send2a, recv2a, y_nbr), exchange(3, send2b, recv2b, x_nbr)]
    core[0].wait()
    r = grp(oy, 0, 2)
    send2a[...] = (acc[r, lo] + recv1[r, lo].astype(f32)).astype(bf16)
    second[0].start()
    core[1].wait()
    for yy in range(2):
        r = grp(yy, ox)
        send2b[yy * group : (yy + 1) * group, :] = (acc[r, hi] + recv1[r, hi].astype(f32)).astype(bf16)
    second[1].start()
    r = grp(y, 0, 2)
    acc[r, lo] = acc[r, lo] + recv1[r, lo].astype(f32)
    for yy in range(2):
        r = grp(yy, x)
        acc[r, hi] = acc[r, hi] + recv1[r, hi].astype(f32)

    def weight_term(left, right, store):
        turned = left[...].T
        for at in range(0, width, STEP):
            size = min(STEP, width - at)
            store(at, size, jnp.dot(turned, right[:, at : at + size], preferred_element_type=f32).astype(bf16))

    def store_at(base):
        def store(at, size, value):
            gw[:, base + at : base + at + size] = value
        return store

    weight_term(gg, xs, store_at(0))

    third = [exchange(4, send3a, recv3a, x_nbr), exchange(5, send3b, recv3b, y_nbr)]
    part = lambda i: pl.ds(pl.multiple_of(i * group, group), group)
    second[0].wait()
    send3a[...] = (acc[grp(y, ox), lo] + recv2a[part(ox), :].astype(f32)).astype(bf16)
    third[0].start()
    second[1].wait()
    send3b[...] = (acc[grp(oy, x), hi] + recv2b[part(oy), :].astype(f32)).astype(bf16)
    third[1].start()
    r = grp(y, x)
    acc[r, lo] = acc[r, lo] + recv2a[part(x), :].astype(f32)
    acc[r, hi] = acc[r, hi] + recv2b[part(y), :].astype(f32)

    weight_term(gu, xs, store_at(width))

    third[0].wait()
    third[1].wait()
    acc[r, lo] = acc[r, lo] + recv3a[...].astype(f32)
    acc[r, hi] = acc[r, hi] + recv3b[...].astype(f32)
    send4[...] = acc[r, :].astype(bf16)
    last = []
    for k in range(1, nz):
        last.append(exchange(5 + k, send4.at[rows(zs[k])], recv4.at[pl.ds((k - 1) * tok, tok)], z_nbrs[k - 1]))
        last[-1].start()

    weight_term(hid, dy, store_at(2 * width))
    store_w = pltpu.make_async_copy(gw, gw_out.at[0], local_sem.at[3])
    store_w.start()

    total = acc[pl.ds(pl.multiple_of((y * 2 + x) * group + z * tok, tok), tok), :]
    for k in range(1, nz):
        last[k - 1].wait()
        total = total + recv4[(k - 1) * tok : k * tok, :].astype(f32)
    gt_out[...] = total.astype(bf16)
    store_w.wait()


def dense_shards(tokens, grad_out, route_ids, route_prob, device_expert, unit_count, expert_weights):
    tok, width = tokens.shape
    devices = lax.axis_size("expert")
    nz = devices // 4
    experts = 5 * devices // 16
    half = expert_weights.shape[1] // lax.axis_size("dp")
    named = route_ids[:, :, None] == jnp.arange(experts, dtype=jnp.int32)[None, None, :]
    scales = jnp.sum(jnp.where(named, route_prob[:, :, None], 0.0), axis=1)
    high = lax.reduce_precision(scales, 8, 7)
    middle = lax.reduce_precision(scales - high, 8, 7)
    spare = 128 - width % 128
    terms = jnp.concatenate([high, middle, scales - high - middle], axis=1).astype(jnp.bfloat16)
    assert 3 * experts <= spare
    terms = jnp.pad(terms, ((0, 0), (0, spare - 3 * experts)))
    padded = width + spare
    grads = jnp.concatenate([grad_out, terms], axis=1)
    position = lax.axis_index("expert")
    expert = lax.dynamic_index_in_dim(device_expert, position, keepdims=False)
    limit = lax.dynamic_index_in_dim(unit_count, position, keepdims=False)
    lane = jnp.arange(128, dtype=jnp.int32) - width % 128
    sel = ((lane >= 0) & (lane < 3 * experts) & (lane % experts == expert)).astype(jnp.float32)[None]
    first = lax.axis_index("dp") * half
    mask = (first + jnp.arange(half, dtype=jnp.int32) < limit).astype(jnp.float32)[None]
    n = 2 * devices * tok
    group = nz * tok
    cut = (width // 128 + 1) // 2 * 128
    rest = width - cut
    bf16, f32 = jnp.bfloat16, jnp.float32
    vmem = pltpu.VMEM
    dma = pltpu.SemaphoreType.DMA
    any_spec = pl.BlockSpec(memory_space=pl.ANY)
    vmem_spec = pl.BlockSpec(memory_space=pltpu.VMEM)
    return pl.pallas_call(
        functools.partial(dense_kernel, nz, half, tok, width),
        out_shape=(
            jax.ShapeDtypeStruct((tok, width), bf16),
            jax.ShapeDtypeStruct((1, half, 3 * width), bf16),
        ),
        in_specs=[any_spec, any_spec, any_spec, vmem_spec, vmem_spec],
        out_specs=(vmem_spec, any_spec),
        scratch_shapes=[
            vmem((n, width), bf16), vmem((n, padded), bf16), vmem((n, width), bf16),
            vmem((half, 3 * width), bf16), vmem((half, width), bf16),
            vmem((n, half), bf16), vmem((n, half), bf16), vmem((n, half), bf16),
            vmem((4 * group, width), f32),
            vmem((4 * group, width), bf16), vmem((4 * group, width), bf16),
            vmem((2 * group, cut), bf16), vmem((2 * group, cut), bf16),
            vmem((2 * group, rest), bf16), vmem((2 * group, rest), bf16),
            vmem((group, cut), bf16), vmem((group, cut), bf16),
            vmem((group, rest), bf16), vmem((group, rest), bf16),
            vmem((group, width), bf16), vmem(((nz - 1) * tok, width), bf16),
            vmem((half, 3 * width), bf16), vmem((16, 128), bf16),
            dma((4,)), dma((2, 2 * devices)), dma((2, nz)), dma((2, 2 * nz)), dma((2, 2 * nz)),
            dma((2, 4 * nz)), dma((5 + nz,)), dma((5 + nz,)),
        ],
        compiler_params=pltpu.CompilerParams(
            collective_id=0, has_side_effects=True, vmem_limit_bytes=60 * 1024 * 1024
        ),
        name="dense_backward",
    )(tokens, grads, expert_weights, sel, mask)


def shards(tokens, grad_out, route_ids, *rest):
    token_count = tokens.shape[0]
    capacity = token_count * route_ids.shape[1] * 4 // lax.axis_size("expert")
    form = dense_shards if capacity >= token_count else routed_shards
    return form(tokens, grad_out, route_ids, *rest)


def solution(mesh):
    in_specs = (P(AXES, None),) * 4 + (P(), P(), P("expert", None, None))
    out_specs = (P(AXES, None), P("expert", "dp", None))
    return jax.shard_map(shards, mesh=mesh, in_specs=in_specs, out_specs=out_specs, check_vma=False)
```

```python
import functools

import jax
import jax.numpy as jnp
from jax import lax
from jax.experimental import pallas as pl
from jax.experimental.pallas import tpu as pltpu
from jax.sharding import PartitionSpec as P

AXES = ("dp", "expert")


def silu_parts(preact):
    sigma = jax.nn.sigmoid(preact)
    return (preact * sigma, sigma * (1.0 + preact * (1.0 - sigma)))


def unit_work(token_rows, grad_rows, slot_weights, unit_mask):
    width = token_rows.shape[1]
    gate_rows = slot_weights[:, :width]
    up_rows = slot_weights[:, width : 2 * width]
    down_rows = slot_weights[:, 2 * width :]
    contract = (((1,), (1,)), ((), ()))
    gate_pre = lax.dot_general(token_rows, gate_rows, contract, preferred_element_type=jnp.float32)
    up_pre = lax.dot_general(token_rows, up_rows, contract, preferred_element_type=jnp.float32)
    back_grad = lax.dot_general(grad_rows, down_rows, contract, preferred_element_type=jnp.float32)
    active, slope = silu_parts(gate_pre)
    hidden = (active * up_pre * unit_mask).astype(jnp.bfloat16)
    grad_gate = (back_grad * up_pre * slope * unit_mask).astype(jnp.bfloat16)
    grad_up = (back_grad * active * unit_mask).astype(jnp.bfloat16)
    partial_value = jnp.dot(grad_gate, gate_rows, preferred_element_type=jnp.float32) + jnp.dot(
        grad_up, up_rows, preferred_element_type=jnp.float32
    )
    return (partial_value, hidden, grad_gate, grad_up)


def weight_terms(token_rows, grad_rows, hidden, grad_gate, grad_up):
    rows_first = (((0,), (0,)), ((), ()))
    return jnp.concatenate(
        [
            lax.dot_general(grad_gate, token_rows, rows_first, preferred_element_type=jnp.float32),
            lax.dot_general(grad_up, token_rows, rows_first, preferred_element_type=jnp.float32),
            lax.dot_general(hidden, grad_rows, rows_first, preferred_element_type=jnp.float32),
        ],
        axis=1,
    )


def send_back(partial_value):
    return lax.all_to_all(partial_value, "expert", split_axis=0, concat_axis=0, tiled=True)


def routed_shards(tokens, grad_out, route_ids, route_prob, device_expert, unit_count, expert_weights):
    token_count, width = tokens.shape
    top_count = route_ids.shape[1]
    devices = lax.axis_size("expert")
    experts = 5 * devices // 16
    capacity = token_count * top_count * 4 // devices
    flat_ids = route_ids.reshape(-1)
    onehot = (flat_ids[:, None] == jnp.arange(experts, dtype=jnp.int32)[None, :]).astype(jnp.int32)
    rank_of = jnp.sum(onehot * jnp.cumsum(onehot, axis=0), axis=1) - 1
    picked = (flat_ids[None, None, :] == device_expert[:, None, None]) & (
        rank_of[None, None, :] == jnp.arange(capacity, dtype=jnp.int32)[None, :, None]
    )
    picked = picked.astype(jnp.float32).reshape(devices * capacity, token_count * top_count)
    by_token = picked.reshape(devices * capacity, token_count, top_count).sum(axis=2)
    route_scale = jnp.dot(picked, route_prob.reshape(-1), precision=lax.Precision.HIGHEST)
    by_token_low = by_token.astype(jnp.bfloat16)
    sent_rows = jnp.dot(by_token_low, tokens, preferred_element_type=jnp.float32).astype(
        jnp.bfloat16
    )
    sent_grads = (
        route_scale[:, None] * jnp.dot(by_token_low, grad_out, preferred_element_type=jnp.float32)
    ).astype(jnp.bfloat16)
    outgoing = jnp.stack([sent_rows, sent_grads], axis=1).reshape(devices, capacity, 2, width)
    position = lax.axis_index("expert")
    unit_limit = lax.dynamic_index_in_dim(unit_count, position, keepdims=False)
    slot_weights = expert_weights[0]
    slot_units = slot_weights.shape[0]
    unit_mask = (jnp.arange(slot_units, dtype=jnp.int32) < unit_limit).astype(jnp.float32)
    arrived = lax.all_to_all(outgoing, "expert", split_axis=0, concat_axis=0, tiled=True)
    row_pairs = arrived.reshape(-1, 2, width)
    partial_value, hidden, grad_gate, grad_up = unit_work(
        row_pairs[:, 0], row_pairs[:, 1], slot_weights, unit_mask
    )
    leading = (arrived.shape[0], arrived.shape[1])
    returned, all_rows, hidden, grad_gate, grad_up = (
        send_back(partial_value.reshape(leading + (width,))),
        arrived,
        hidden.reshape(leading + (slot_units,)),
        grad_gate.reshape(leading + (slot_units,)),
        grad_up.reshape(leading + (slot_units,)),
    )
    row_pairs = all_rows.reshape(-1, 2, width)
    token_rows = row_pairs[:, 0]
    grad_rows = row_pairs[:, 1]
    hidden = hidden.reshape(-1, slot_units)
    grad_gate = grad_gate.reshape(-1, slot_units)
    grad_up = grad_up.reshape(-1, slot_units)
    term_block = weight_terms(token_rows, grad_rows, hidden, grad_gate, grad_up)
    grad_weights = lax.psum_scatter(term_block, "dp", scatter_dimension=0, tiled=True)
    parts = returned.reshape(devices * capacity, width)
    grad_tokens = lax.dot_general(
        by_token,
        parts,
        (((0,), (0,)), ((), ())),
        precision=lax.Precision.HIGHEST,
        preferred_element_type=jnp.float32,
    )
    return (grad_tokens.astype(jnp.bfloat16), grad_weights.astype(jnp.bfloat16)[None])


MESH = pl.DeviceIdType.MESH
STEP = 256


def dense_kernel(
    nz, half, tok, width, experts,
    x_in, g_in, w_in, ids_ref, prob_ref, expert_ref, limit_ref, gt_out, gw_out,
    xs, gs, dy, w, wu, gg, gu, hid, acc, send1, recv1, send2a, recv2a, send2b, recv2b,
    send3a, recv3a, send3b, recv3b, send4, recv4, gw, up,
    local_sem, recv_sem, sz, sx, sy, ss, rs_send, rs_recv,
):
    f32, bf16 = jnp.float32, jnp.bfloat16
    y = lax.axis_index("dp")
    position = lax.axis_index("expert")
    z, x, c = position // 4, (position // 2) % 2, position % 2
    oy, ox, oc = 1 - y, 1 - x, 1 - c

    def place(yy, zz, xx, cc):
        return (yy, zz * 4 + xx * 2 + cc)

    def slot(cc, yy, xx, zz):
        return ((cc * 2 + yy) * 2 + xx) * nz + zz

    def rows(s, count=1):
        return pl.ds(pl.multiple_of(s * tok, tok), count * tok)

    zs = [lax.rem(z + k, nz) for k in range(nz)]
    x_nbr, y_nbr, sib = place(y, z, ox, c), place(oy, z, x, c), place(y, z, x, oc)
    z_nbrs = [place(y, zs[k], x, c) for k in range(1, nz)]
    z_sides = (place(y, lax.rem(z + nz - 1, nz), x, c), place(y, lax.rem(z + 1, nz), x, c))
    has_side = (z > 0, z < nz - 1)

    mine = slot(c, y, x, z)
    first = pl.multiple_of(y * half, 16)
    own_x = pltpu.make_async_copy(x_in, xs.at[rows(mine)], local_sem.at[0])
    load_w = pltpu.make_async_copy(w_in.at[0, pl.ds(first, half)], w, local_sem.at[2])
    for copy in (own_x, load_w):
        copy.start()
    barrier = pltpu.get_barrier_semaphore()
    peers = [x_nbr, y_nbr, sib] + z_nbrs
    for peer in peers:
        pl.semaphore_signal(barrier, inc=1, device_id=peer, device_id_type=MESH)

    spare = gs.shape[1] - width
    lane = lax.broadcasted_iota(jnp.int32, (tok, spare), 1)
    scales = jnp.zeros((tok, spare), f32)
    for k in range(ids_ref.shape[1]):
        scales += jnp.where(ids_ref[:, k : k + 1] == lane % experts, prob_ref[:, k : k + 1], 0.0)
    high = scales.astype(bf16).astype(f32)
    middle = (scales - high).astype(bf16).astype(f32)
    term = lane // experts
    packed = jnp.where(term == 0, high, jnp.where(term == 1, middle, scales - high - middle))
    gs[rows(mine), :width] = g_in[...]
    gs[rows(mine), width:] = jnp.where(term < 3, packed, 0.0).astype(bf16)
    own_x.wait()
    pl.semaphore_wait(barrier, len(peers))

    bufs = (xs, gs)

    def describe(p, s, target, sem):
        return pltpu.make_async_remote_copy(
            src_ref=bufs[p].at[rows(s)], dst_ref=bufs[p].at[rows(s)],
            send_sem=sem, recv_sem=recv_sem.at[p, s], device_id=target, device_id_type=MESH,
        )

    def arrived(p, s):
        describe(p, s, sib, ss.at[p, 0]).wait_recv()

    def along_z(p, zz, side):
        return describe(p, slot(c, y, x, zz), z_sides[side], sz.at[p, side, zz])

    def to_x(p, yy, zz):
        return describe(p, slot(c, yy, x, zz), x_nbr, sx.at[p, (yy if p else 0) * nz + zz])

    def to_y(p, xx, zz):
        return describe(p, slot(c, y, xx, zz), y_nbr, sy.at[p, (0 if p else xx) * nz + zz])

    def to_sib(p, yy, xx, zz):
        return describe(p, slot(c, yy, xx, zz), sib, ss.at[p, (yy * 2 + xx) * nz + zz])

    def spread(p, zz):
        to_x(p, y, zz).start()
        to_y(p, x, zz).start()
        to_sib(p, y, x, zz).start()

    def relay(zz):
        arrived(0, slot(c, y, ox, zz))
        to_y(0, ox, zz).start()
        to_sib(0, y, ox, zz).start()
        arrived(1, slot(c, oy, x, zz))
        to_x(1, oy, zz).start()
        to_sib(1, oy, x, zz).start()

    def at_distance(d, act):
        for side, zz in ((0, z - d), (1, z + d)):
            pl.when((zz >= 0) & (zz < nz))(functools.partial(act, side, zz))

    def from_z(side, zz):
        for p in range(2):
            arrived(p, slot(c, y, x, zz))
            pl.when(has_side[1 - side])(lambda: along_z(p, zz, 1 - side).start())
            spread(p, zz)

    for p in range(2):
        for side in range(2):
            pl.when(has_side[side])(lambda: along_z(p, z, side).start())
        spread(p, z)
    for d in range(1, nz):
        at_distance(d, from_z)
        if d == 1:
            relay(z)
        else:
            at_distance(d - 1, lambda side, zz: relay(zz))
    at_distance(nz - 1, lambda side, zz: relay(zz))
    load_w.wait()
    wu[...] = w[:, width : 2 * width]

    def finish(zz):
        for p, yy, xx in ((0, oy, x), (1, y, ox), (0, oy, ox), (1, oy, ox)):
            arrived(p, slot(c, yy, xx, zz))
            to_sib(p, yy, xx, zz).start()

    finish(z)
    for d in range(1, nz):
        at_distance(d, lambda side, zz: finish(zz))
    for k in range(nz):
        for yy in range(2):
            for xx in range(2):
                for p in range(2):
                    arrived(p, slot(oc, yy, xx, k))

    def drain_z(side, zz):
        for p in range(2):
            pl.when(has_side[1 - side])(lambda: along_z(p, zz, 1 - side).wait_send())

    for p in range(2):
        for side in range(2):
            pl.when(has_side[side])(lambda: along_z(p, z, side).wait_send())
    for d in range(1, nz):
        at_distance(d, drain_z)
    for k in range(nz):
        for p in range(2):
            to_x(p, y, k).wait_send()
            to_y(p, x, k).wait_send()
            for yy in range(2):
                for xx in range(2):
                    to_sib(p, yy, xx, k).wait_send()
        to_y(0, ox, k).wait_send()
        to_x(1, oy, k).wait_send()

    expert = expert_ref[position]
    lane = lax.broadcasted_iota(jnp.int32, (1, 128), 1) - (128 - spare)
    sel = jnp.where((lane >= 0) & (lane < 3 * experts) & (lane % experts == expert), 1.0, 0.0)
    unit = lax.broadcasted_iota(jnp.int32, (1, half), 1) + y * half
    unit_mask = jnp.where(unit < limit_ref[position], 1.0, 0.0)
    contract = (((1,), (1,)), ((), ()))
    block = 4 * nz * tok // 2
    tail = width // 128 * 128

    def forward(i, carry):
        r = pl.ds(pl.multiple_of(i * block, block), block)
        scale = jnp.sum(gs[r, tail:].astype(f32) * sel, axis=1, keepdims=True)
        dy[r, :] = (scale * gs[r, :width].astype(f32)).astype(bf16)
        token_rows = xs[r, :]
        g = lax.dot_general(token_rows, w[:, :width], contract, preferred_element_type=f32)
        v = lax.dot_general(token_rows, wu[...], contract, preferred_element_type=f32)
        b = lax.dot_general(dy[r, :], w[:, 2 * width :], contract, preferred_element_type=f32)
        live = jnp.broadcast_to(unit_mask, g.shape) > 0.0
        sigma = 1.0 / (1.0 + jnp.exp(-g))
        active = g * sigma
        hid[r, :] = jnp.where(live, active * v, 0.0).astype(bf16)
        gg[r, :] = jnp.where(live, b * v * (sigma * (1.0 + g * (1.0 - sigma))), 0.0).astype(bf16)
        gu[r, :] = jnp.where(live, b * active, 0.0).astype(bf16)
        return carry

    lax.fori_loop(0, 8 * nz * tok // block, forward, 0)

    group = nz * tok
    all_rows = 4 * group
    cut = (width // 128 + 1) // 2 * 128
    half_cols = (pl.ds(0, cut), pl.ds(cut, width - cut))
    spans = [(at, min(STEP, end - at)) for begin, end in ((0, cut), (cut, width)) for at in range(begin, end, STEP)]

    def partial(side, at, size):
        r = pl.ds(pl.multiple_of(side * all_rows, all_rows), all_rows)
        return jnp.dot(gg[r, :], w[:, at : at + size], preferred_element_type=f32) + jnp.dot(
            gu[r, :], wu[:, at : at + size], preferred_element_type=f32
        )

    def exchange(index, src, dst, target):
        return pltpu.make_async_remote_copy(
            src_ref=src, dst_ref=dst, send_sem=rs_send.at[index], recv_sem=rs_recv.at[index],
            device_id=target, device_id_type=MESH,
        )

    core = [exchange(h, send1.at[:, half_cols[h]], recv1.at[:, half_cols[h]], sib) for h in range(2)]
    for at, size in spans:
        send1[:, at : at + size] = partial(oc, at, size).astype(bf16)
        if at + size == cut:
            core[0].start()
    core[1].start()
    for at, size in spans:
        acc[:, at : at + size] = partial(c, at, size)

    def grp(yy, xx, count=1):
        return pl.ds(pl.multiple_of((yy * 2 + xx) * group, group), count * group)

    lo, hi = slice(0, cut), slice(cut, width)
    second = [exchange(2, send2a, recv2a, y_nbr), exchange(3, send2b, recv2b, x_nbr)]
    core[0].wait()
    r = grp(oy, 0, 2)
    send2a[...] = (acc[r, lo] + recv1[r, lo].astype(f32)).astype(bf16)
    second[0].start()
    core[1].wait()
    for yy in range(2):
        r = grp(yy, ox)
        send2b[yy * group : (yy + 1) * group, :] = (acc[r, hi] + recv1[r, hi].astype(f32)).astype(bf16)
    second[1].start()
    r = grp(y, 0, 2)
    acc[r, lo] = acc[r, lo] + recv1[r, lo].astype(f32)
    for yy in range(2):
        r = grp(yy, x)
        acc[r, hi] = acc[r, hi] + recv1[r, hi].astype(f32)

    def weight_term(left, right, store):
        turned = left[...].T
        for at in range(0, width, STEP):
            size = min(STEP, width - at)
            store(at, size, jnp.dot(turned, right[:, at : at + size], preferred_element_type=f32).astype(bf16))

    def store_at(base):
        def store(at, size, value):
            gw[:, base + at : base + at + size] = value
        return store

    weight_term(gg, xs, store_at(0))

    third = [exchange(4, send3a, recv3a, x_nbr), exchange(5, send3b, recv3b, y_nbr)]
    part = lambda i: pl.ds(pl.multiple_of(i * group, group), group)
    second[0].wait()
    send3a[...] = (acc[grp(y, ox), lo] + recv2a[part(ox), :].astype(f32)).astype(bf16)
    third[0].start()
    second[1].wait()
    send3b[...] = (acc[grp(oy, x), hi] + recv2b[part(oy), :].astype(f32)).astype(bf16)
    third[1].start()
    r = grp(y, x)
    acc[r, lo] = acc[r, lo] + recv2a[part(x), :].astype(f32)
    acc[r, hi] = acc[r, hi] + recv2b[part(y), :].astype(f32)

    weight_term(gu, xs, store_at(width))

    third[0].wait()
    third[1].wait()
    acc[r, lo] = acc[r, lo] + recv3a[...].astype(f32)
    acc[r, hi] = acc[r, hi] + recv3b[...].astype(f32)
    send4[...] = acc[r, :].astype(bf16)
    last = []
    for k in range(1, nz):
        last.append(exchange(5 + k, send4.at[rows(zs[k])], recv4.at[pl.ds((k - 1) * tok, tok)], z_nbrs[k - 1]))
        last[-1].start()

    weight_term(hid, dy, store_at(2 * width))
    store_w = pltpu.make_async_copy(gw, gw_out.at[0], local_sem.at[3])
    store_w.start()

    total = acc[pl.ds(pl.multiple_of((y * 2 + x) * group + z * tok, tok), tok), :]
    for k in range(1, nz):
        last[k - 1].wait()
        total = total + recv4[(k - 1) * tok : k * tok, :].astype(f32)
    gt_out[...] = total.astype(bf16)
    store_w.wait()


def dense_shards(tokens, grad_out, route_ids, route_prob, device_expert, unit_count, expert_weights):
    tok, width = tokens.shape
    devices = lax.axis_size("expert")
    nz = devices // 4
    experts = 5 * devices // 16
    half = expert_weights.shape[1] // lax.axis_size("dp")
    spare = 128 - width % 128
    assert 3 * experts <= spare
    padded = width + spare
    n = 2 * devices * tok
    group = nz * tok
    cut = (width // 128 + 1) // 2 * 128
    rest = width - cut
    bf16, f32 = jnp.bfloat16, jnp.float32
    vmem = pltpu.VMEM
    dma = pltpu.SemaphoreType.DMA
    any_spec = pl.BlockSpec(memory_space=pl.ANY)
    smem_spec = pl.BlockSpec(memory_space=pltpu.SMEM)
    vmem_spec = pl.BlockSpec(memory_space=pltpu.VMEM)
    return pl.pallas_call(
        functools.partial(dense_kernel, nz, half, tok, width, experts),
        out_shape=(
            jax.ShapeDtypeStruct((tok, width), bf16),
            jax.ShapeDtypeStruct((1, half, 3 * width), bf16),
        ),
        in_specs=[any_spec, vmem_spec, any_spec, vmem_spec, vmem_spec, smem_spec, smem_spec],
        out_specs=(vmem_spec, any_spec),
        scratch_shapes=[
            vmem((n, width), bf16), vmem((n, padded), bf16), vmem((n, width), bf16),
            vmem((half, 3 * width), bf16), vmem((half, width), bf16),
            vmem((n, half), bf16), vmem((n, half), bf16), vmem((n, half), bf16),
            vmem((4 * group, width), f32),
            vmem((4 * group, width), bf16), vmem((4 * group, width), bf16),
            vmem((2 * group, cut), bf16), vmem((2 * group, cut), bf16),
            vmem((2 * group, rest), bf16), vmem((2 * group, rest), bf16),
            vmem((group, cut), bf16), vmem((group, cut), bf16),
            vmem((group, rest), bf16), vmem((group, rest), bf16),
            vmem((group, width), bf16), vmem(((nz - 1) * tok, width), bf16),
            vmem((half, 3 * width), bf16), vmem((16, 128), bf16),
            dma((4,)), dma((2, 2 * devices)), dma((2, 2, nz)), dma((2, 2 * nz)), dma((2, 2 * nz)),
            dma((2, 4 * nz)), dma((5 + nz,)), dma((5 + nz,)),
        ],
        compiler_params=pltpu.CompilerParams(
            collective_id=0, has_side_effects=True, vmem_limit_bytes=60 * 1024 * 1024
        ),
        name="dense_backward",
    )(tokens, grad_out, expert_weights, route_ids, route_prob, device_expert, unit_count)


def shards(tokens, grad_out, route_ids, *rest):
    token_count = tokens.shape[0]
    capacity = token_count * route_ids.shape[1] * 4 // lax.axis_size("expert")
    form = dense_shards if capacity >= token_count else routed_shards
    return form(tokens, grad_out, route_ids, *rest)


def solution(mesh):
    in_specs = (P(AXES, None),) * 4 + (P(), P(), P("expert", None, None))
    out_specs = (P(AXES, None), P("expert", "dp", None))
    return jax.shard_map(shards, mesh=mesh, in_specs=in_specs, out_specs=out_specs, check_vma=False)
```

```python
import functools

import jax
import jax.numpy as jnp
from jax import lax
from jax.experimental import pallas as pl
from jax.experimental.pallas import tpu as pltpu
from jax.sharding import PartitionSpec as P

AXES = ("dp", "expert")


def silu_parts(preact):
    sigma = jax.nn.sigmoid(preact)
    return (preact * sigma, sigma * (1.0 + preact * (1.0 - sigma)))


def unit_work(token_rows, grad_rows, slot_weights, unit_mask):
    width = token_rows.shape[1]
    gate_rows = slot_weights[:, :width]
    up_rows = slot_weights[:, width : 2 * width]
    down_rows = slot_weights[:, 2 * width :]
    contract = (((1,), (1,)), ((), ()))
    gate_pre = lax.dot_general(token_rows, gate_rows, contract, preferred_element_type=jnp.float32)
    up_pre = lax.dot_general(token_rows, up_rows, contract, preferred_element_type=jnp.float32)
    back_grad = lax.dot_general(grad_rows, down_rows, contract, preferred_element_type=jnp.float32)
    active, slope = silu_parts(gate_pre)
    hidden = (active * up_pre * unit_mask).astype(jnp.bfloat16)
    grad_gate = (back_grad * up_pre * slope * unit_mask).astype(jnp.bfloat16)
    grad_up = (back_grad * active * unit_mask).astype(jnp.bfloat16)
    partial_value = jnp.dot(grad_gate, gate_rows, preferred_element_type=jnp.float32) + jnp.dot(
        grad_up, up_rows, preferred_element_type=jnp.float32
    )
    return (partial_value, hidden, grad_gate, grad_up)


def weight_terms(token_rows, grad_rows, hidden, grad_gate, grad_up):
    rows_first = (((0,), (0,)), ((), ()))
    return jnp.concatenate(
        [
            lax.dot_general(grad_gate, token_rows, rows_first, preferred_element_type=jnp.float32),
            lax.dot_general(grad_up, token_rows, rows_first, preferred_element_type=jnp.float32),
            lax.dot_general(hidden, grad_rows, rows_first, preferred_element_type=jnp.float32),
        ],
        axis=1,
    )


def send_back(partial_value):
    return lax.all_to_all(partial_value, "expert", split_axis=0, concat_axis=0, tiled=True)


def routed_shards(tokens, grad_out, route_ids, route_prob, device_expert, unit_count, expert_weights):
    token_count, width = tokens.shape
    top_count = route_ids.shape[1]
    devices = lax.axis_size("expert")
    experts = 5 * devices // 16
    capacity = token_count * top_count * 4 // devices
    flat_ids = route_ids.reshape(-1)
    onehot = (flat_ids[:, None] == jnp.arange(experts, dtype=jnp.int32)[None, :]).astype(jnp.int32)
    rank_of = jnp.sum(onehot * jnp.cumsum(onehot, axis=0), axis=1) - 1
    picked = (flat_ids[None, None, :] == device_expert[:, None, None]) & (
        rank_of[None, None, :] == jnp.arange(capacity, dtype=jnp.int32)[None, :, None]
    )
    picked = picked.astype(jnp.float32).reshape(devices * capacity, token_count * top_count)
    by_token = picked.reshape(devices * capacity, token_count, top_count).sum(axis=2)
    route_scale = jnp.dot(picked, route_prob.reshape(-1), precision=lax.Precision.HIGHEST)
    by_token_low = by_token.astype(jnp.bfloat16)
    sent_rows = jnp.dot(by_token_low, tokens, preferred_element_type=jnp.float32).astype(
        jnp.bfloat16
    )
    sent_grads = (
        route_scale[:, None] * jnp.dot(by_token_low, grad_out, preferred_element_type=jnp.float32)
    ).astype(jnp.bfloat16)
    outgoing = jnp.stack([sent_rows, sent_grads], axis=1).reshape(devices, capacity, 2, width)
    position = lax.axis_index("expert")
    unit_limit = lax.dynamic_index_in_dim(unit_count, position, keepdims=False)
    slot_weights = expert_weights[0]
    slot_units = slot_weights.shape[0]
    unit_mask = (jnp.arange(slot_units, dtype=jnp.int32) < unit_limit).astype(jnp.float32)
    arrived = lax.all_to_all(outgoing, "expert", split_axis=0, concat_axis=0, tiled=True)
    row_pairs = arrived.reshape(-1, 2, width)
    partial_value, hidden, grad_gate, grad_up = unit_work(
        row_pairs[:, 0], row_pairs[:, 1], slot_weights, unit_mask
    )
    leading = (arrived.shape[0], arrived.shape[1])
    returned, all_rows, hidden, grad_gate, grad_up = (
        send_back(partial_value.reshape(leading + (width,))),
        arrived,
        hidden.reshape(leading + (slot_units,)),
        grad_gate.reshape(leading + (slot_units,)),
        grad_up.reshape(leading + (slot_units,)),
    )
    row_pairs = all_rows.reshape(-1, 2, width)
    token_rows = row_pairs[:, 0]
    grad_rows = row_pairs[:, 1]
    hidden = hidden.reshape(-1, slot_units)
    grad_gate = grad_gate.reshape(-1, slot_units)
    grad_up = grad_up.reshape(-1, slot_units)
    term_block = weight_terms(token_rows, grad_rows, hidden, grad_gate, grad_up)
    grad_weights = lax.psum_scatter(term_block, "dp", scatter_dimension=0, tiled=True)
    parts = returned.reshape(devices * capacity, width)
    grad_tokens = lax.dot_general(
        by_token,
        parts,
        (((0,), (0,)), ((), ())),
        precision=lax.Precision.HIGHEST,
        preferred_element_type=jnp.float32,
    )
    return (grad_tokens.astype(jnp.bfloat16), grad_weights.astype(jnp.bfloat16)[None])


MESH = pl.DeviceIdType.MESH
STEP = 256


def dense_kernel(
    nz, half, tok, width, experts,
    x_in, g_in, w_in, ids_ref, prob_ref, expert_ref, limit_ref, gt_out, gw_out,
    xs, gs, dy, w, wu, gate_pre, up_pre, gg, gu, hid, acc, send1, recv1, send2, recv2,
    send3, recv3, send4, recv4, gw,
    local_sem, recv_sem, sz, sx, sy, ss, rs_send, rs_recv,
):
    f32, bf16 = jnp.float32, jnp.bfloat16
    y = lax.axis_index("dp")
    position = lax.axis_index("expert")
    z, x, c = position // 4, (position // 2) % 2, position % 2
    oy, ox, oc = 1 - y, 1 - x, 1 - c

    def place(yy, zz, xx, cc):
        return (yy, zz * 4 + xx * 2 + cc)

    def slot(cc, yy, xx, zz):
        return ((cc * 2 + yy) * 2 + xx) * nz + zz

    def rows(s, count=1):
        return pl.ds(pl.multiple_of(s * tok, tok), count * tok)

    zs = [lax.rem(z + k, nz) for k in range(nz)]
    x_nbr, y_nbr, sib = place(y, z, ox, c), place(oy, z, x, c), place(y, z, x, oc)
    z_nbrs = [place(y, zs[k], x, c) for k in range(1, nz)]
    z_sides = (place(y, lax.rem(z + nz - 1, nz), x, c), place(y, lax.rem(z + 1, nz), x, c))
    has_side = (z > 0, z < nz - 1)

    mine = slot(c, y, x, z)
    first = pl.multiple_of(y * half, 16)
    own_x = pltpu.make_async_copy(x_in, xs.at[rows(mine)], local_sem.at[0])
    load_w = pltpu.make_async_copy(w_in.at[0, pl.ds(first, half)], w, local_sem.at[2])
    for copy in (own_x, load_w):
        copy.start()
    barrier = pltpu.get_barrier_semaphore()
    peers = [x_nbr, y_nbr, sib] + z_nbrs
    for peer in peers:
        pl.semaphore_signal(barrier, inc=1, device_id=peer, device_id_type=MESH)

    spare = gs.shape[1] - width
    lane = lax.broadcasted_iota(jnp.int32, (tok, spare), 1)
    scales = jnp.zeros((tok, spare), f32)
    for k in range(ids_ref.shape[1]):
        scales += jnp.where(ids_ref[:, k : k + 1] == lane % experts, prob_ref[:, k : k + 1], 0.0)
    high = scales.astype(bf16).astype(f32)
    middle = (scales - high).astype(bf16).astype(f32)
    term = lane // experts
    packed = jnp.where(term == 0, high, jnp.where(term == 1, middle, scales - high - middle))
    gs[rows(mine), :width] = g_in[...]
    gs[rows(mine), width:] = jnp.where(term < 3, packed, 0.0).astype(bf16)
    own_x.wait()
    pl.semaphore_wait(barrier, len(peers))

    bufs = (xs, gs)

    def describe(p, s, target, sem):
        return pltpu.make_async_remote_copy(
            src_ref=bufs[p].at[rows(s)], dst_ref=bufs[p].at[rows(s)],
            send_sem=sem, recv_sem=recv_sem.at[p, s], device_id=target, device_id_type=MESH,
        )

    def arrived(p, s):
        describe(p, s, sib, ss.at[p, 0]).wait_recv()

    def along_z(p, zz, side):
        return describe(p, slot(c, y, x, zz), z_sides[side], sz.at[p, side, zz])

    def to_x(p, yy, zz):
        return describe(p, slot(c, yy, x, zz), x_nbr, sx.at[p, (yy if p else 0) * nz + zz])

    def to_y(p, xx, zz):
        return describe(p, slot(c, y, xx, zz), y_nbr, sy.at[p, (0 if p else xx) * nz + zz])

    def to_sib(p, yy, xx, zz):
        return describe(p, slot(c, yy, xx, zz), sib, ss.at[p, (yy * 2 + xx) * nz + zz])

    def spread(p, zz):
        to_x(p, y, zz).start()
        to_y(p, x, zz).start()
        to_sib(p, y, x, zz).start()

    def relay(zz):
        arrived(0, slot(c, y, ox, zz))
        to_y(0, ox, zz).start()
        to_sib(0, y, ox, zz).start()
        arrived(1, slot(c, oy, x, zz))
        to_x(1, oy, zz).start()
        to_sib(1, oy, x, zz).start()

    def at_distance(d, act):
        for side, zz in ((0, z - d), (1, z + d)):
            pl.when((zz >= 0) & (zz < nz))(functools.partial(act, side, zz))

    def from_z(side, zz):
        for p in range(2):
            arrived(p, slot(c, y, x, zz))
            pl.when(has_side[1 - side])(lambda: along_z(p, zz, 1 - side).start())
            spread(p, zz)

    for p in range(2):
        for side in range(2):
            pl.when(has_side[side])(lambda: along_z(p, z, side).start())
        spread(p, z)
    for d in range(1, nz):
        at_distance(d, from_z)
        if d == 1:
            relay(z)
        else:
            at_distance(d - 1, lambda side, zz: relay(zz))
    at_distance(nz - 1, lambda side, zz: relay(zz))
    expert = expert_ref[position]
    lane = lax.broadcasted_iota(jnp.int32, (1, 128), 1) - (128 - spare)
    sel = jnp.where((lane >= 0) & (lane < 3 * experts) & (lane % experts == expert), 1.0, 0.0)
    unit = lax.broadcasted_iota(jnp.int32, (1, half), 1) + y * half
    unit_mask = jnp.where(unit < limit_ref[position], 1.0, 0.0)
    contract = (((1,), (1,)), ((), ()))
    block = 2 * nz * tok
    tail = width // 128 * 128

    def block_rows(cc, yy):
        return pl.ds(pl.multiple_of((cc * 2 + yy) * block, block), block)

    def gate_up(cc, yy):
        r = block_rows(cc, yy)
        gate_pre[r, :] = lax.dot_general(xs[r, :], w[:, :width], contract, preferred_element_type=f32)
        up_pre[r, :] = lax.dot_general(xs[r, :], wu[...], contract, preferred_element_type=f32)

    def backward(cc, yy):
        r = block_rows(cc, yy)
        scale = jnp.sum(gs[r, tail:].astype(f32) * sel, axis=1, keepdims=True)
        dy[r, :] = (scale * gs[r, :width].astype(f32)).astype(bf16)
        b = lax.dot_general(dy[r, :], w[:, 2 * width :], contract, preferred_element_type=f32)
        g, v = gate_pre[r, :], up_pre[r, :]
        live = jnp.broadcast_to(unit_mask, g.shape) > 0.0
        sigma = 1.0 / (1.0 + jnp.exp(-g))
        active = g * sigma
        hid[r, :] = jnp.where(live, active * v, 0.0).astype(bf16)
        gg[r, :] = jnp.where(live, b * v * (sigma * (1.0 + g * (1.0 - sigma))), 0.0).astype(bf16)
        gu[r, :] = jnp.where(live, b * active, 0.0).astype(bf16)

    load_w.wait()
    wu[...] = w[:, width : 2 * width]
    gate_up(c, y)

    def finish(zz):
        for p, yy, xx in ((0, oy, x), (1, y, ox), (0, oy, ox), (1, oy, ox)):
            arrived(p, slot(c, yy, xx, zz))
            to_sib(p, yy, xx, zz).start()

    finish(z)
    for d in range(1, nz - 1):
        at_distance(d, lambda side, zz: finish(zz))
    for k in range(nz):
        for xx in range(2):
            arrived(0, slot(oc, y, xx, k))
    gate_up(oc, y)
    at_distance(nz - 1, lambda side, zz: finish(zz))
    gate_up(c, oy)
    backward(c, y)
    backward(c, oy)
    for k in range(nz):
        for xx in range(2):
            arrived(0, slot(oc, oy, xx, k))
            arrived(1, slot(oc, y, xx, k))
            arrived(1, slot(oc, oy, xx, k))
    gate_up(oc, oy)
    backward(oc, y)
    backward(oc, oy)

    group = nz * tok
    all_rows = 4 * group
    quarter = (width // 128 + 4) // 4 * 128
    strips = [(at, min(at + quarter, width)) for at in range(0, width, quarter)]
    count = len(strips)

    def spans(begin, end):
        return [(at, min(STEP, end - at)) for at in range(begin, end, STEP)]

    def partial(side, at, size):
        r = pl.ds(pl.multiple_of(side * all_rows, all_rows), all_rows)
        return jnp.dot(gg[r, :], w[:, at : at + size], preferred_element_type=f32) + jnp.dot(
            gu[r, :], wu[:, at : at + size], preferred_element_type=f32
        )

    def exchange(index, src, dst, target):
        return pltpu.make_async_remote_copy(
            src_ref=src, dst_ref=dst, send_sem=rs_send.at[index], recv_sem=rs_recv.at[index],
            device_id=target, device_id_type=MESH,
        )

    def grp(yy, xx):
        return pl.ds(pl.multiple_of((yy * 2 + xx) * group, group), group)

    def part(i):
        return pl.ds(pl.multiple_of(i * group, group), group)

    def strip_ref(ref, i):
        begin, end = strips[i]
        return ref.at[:, pl.ds(begin, end - begin)]

    core, second, third, last = [], [], [], []
    for i in range(count):
        even = i % 2 == 0
        core.append(exchange(i, strip_ref(send1, i), strip_ref(recv1, i), sib))
        second.append(exchange(count + i, strip_ref(send2, i), strip_ref(recv2, i), y_nbr if even else x_nbr))
        third.append(exchange(2 * count + i, strip_ref(send3, i), strip_ref(recv3, i), x_nbr if even else y_nbr))

    for i, (begin, end) in enumerate(strips):
        for at, size in spans(begin, end):
            send1[:, at : at + size] = partial(oc, at, size).astype(bf16)
        core[i].start()

    def second_stage(i):
        begin, end = strips[i]
        cols = slice(begin, end)
        for at, size in spans(begin, end):
            acc[:, at : at + size] = partial(c, at, size)
        core[i].wait()
        for j in range(2):
            r = grp(oy, j) if i % 2 == 0 else grp(j, ox)
            send2[j * group : (j + 1) * group, cols] = (acc[r, cols] + recv1[r, cols].astype(f32)).astype(bf16)
        second[i].start()
        for j in range(2):
            r = grp(y, j) if i % 2 == 0 else grp(j, x)
            acc[r, cols] = acc[r, cols] + recv1[r, cols].astype(f32)

    def third_stage(i):
        cols = slice(*strips[i])
        away, stay, r = (ox, x, grp(y, ox)) if i % 2 == 0 else (oy, y, grp(oy, x))
        second[i].wait()
        send3[:, cols] = (acc[r, cols] + recv2[part(away), cols].astype(f32)).astype(bf16)
        third[i].start()
        r = grp(y, x)
        acc[r, cols] = acc[r, cols] + recv2[part(stay), cols].astype(f32)

    def last_stage(i):
        begin, end = strips[i]
        cols = slice(begin, end)
        r = grp(y, x)
        third[i].wait()
        acc[r, cols] = acc[r, cols] + recv3[:, cols].astype(f32)
        send4[:, cols] = acc[r, cols].astype(bf16)
        for k in range(1, nz):
            copy = exchange(
                3 * count + i * (nz - 1) + k - 1,
                send4.at[rows(zs[k]), pl.ds(begin, end - begin)],
                recv4.at[pl.ds((k - 1) * tok, tok), pl.ds(begin, end - begin)],
                z_nbrs[k - 1],
            )
            copy.start()
            last.append(copy)

    def weight_term(left, right, base):
        turned = left[...].T
        for at, size in spans(0, width):
            value = jnp.dot(turned, right[:, at : at + size], preferred_element_type=f32)
            gw[:, base + at : base + at + size] = value.astype(bf16)

    for i in range(count):
        second_stage(i)
    weight_term(gg, xs, 0)
    for i in range(count):
        third_stage(i)
        if i == 1:
            weight_term(gu, xs, width)
    for i in range(count):
        last_stage(i)
    weight_term(hid, dy, 2 * width)
    store_w = pltpu.make_async_copy(gw, gw_out.at[0], local_sem.at[3])
    store_w.start()

    def drain_z(side, zz):
        for p in range(2):
            pl.when(has_side[1 - side])(lambda: along_z(p, zz, 1 - side).wait_send())

    for p in range(2):
        for side in range(2):
            pl.when(has_side[side])(lambda: along_z(p, z, side).wait_send())
    for d in range(1, nz):
        at_distance(d, drain_z)
    for k in range(nz):
        for p in range(2):
            to_x(p, y, k).wait_send()
            to_y(p, x, k).wait_send()
            for yy in range(2):
                for xx in range(2):
                    to_sib(p, yy, xx, k).wait_send()
        to_y(0, ox, k).wait_send()
        to_x(1, oy, k).wait_send()

    total = acc[pl.ds(pl.multiple_of((y * 2 + x) * group + z * tok, tok), tok), :]
    for copy in last:
        copy.wait()
    for k in range(1, nz):
        total = total + recv4[(k - 1) * tok : k * tok, :].astype(f32)
    gt_out[...] = total.astype(bf16)
    store_w.wait()


def dense_shards(tokens, grad_out, route_ids, route_prob, device_expert, unit_count, expert_weights):
    tok, width = tokens.shape
    devices = lax.axis_size("expert")
    nz = devices // 4
    experts = 5 * devices // 16
    half = expert_weights.shape[1] // lax.axis_size("dp")
    spare = 128 - width % 128
    assert 3 * experts <= spare
    padded = width + spare
    n = 2 * devices * tok
    group = nz * tok
    bf16, f32 = jnp.bfloat16, jnp.float32
    vmem = pltpu.VMEM
    dma = pltpu.SemaphoreType.DMA
    any_spec = pl.BlockSpec(memory_space=pl.ANY)
    smem_spec = pl.BlockSpec(memory_space=pltpu.SMEM)
    vmem_spec = pl.BlockSpec(memory_space=pltpu.VMEM)
    return pl.pallas_call(
        functools.partial(dense_kernel, nz, half, tok, width, experts),
        out_shape=(
            jax.ShapeDtypeStruct((tok, width), bf16),
            jax.ShapeDtypeStruct((1, half, 3 * width), bf16),
        ),
        in_specs=[any_spec, vmem_spec, any_spec, vmem_spec, vmem_spec, smem_spec, smem_spec],
        out_specs=(vmem_spec, any_spec),
        scratch_shapes=[
            vmem((n, width), bf16), vmem((n, padded), bf16), vmem((n, width), bf16),
            vmem((half, 3 * width), bf16), vmem((half, width), bf16),
            vmem((n, half), f32), vmem((n, half), f32),
            vmem((n, half), bf16), vmem((n, half), bf16), vmem((n, half), bf16),
            vmem((4 * group, width), f32),
            vmem((4 * group, width), bf16), vmem((4 * group, width), bf16),
            vmem((2 * group, width), bf16), vmem((2 * group, width), bf16),
            vmem((group, width), bf16), vmem((group, width), bf16),
            vmem((group, width), bf16), vmem(((nz - 1) * tok, width), bf16),
            vmem((half, 3 * width), bf16),
            dma((4,)), dma((2, 2 * devices)), dma((2, 2, nz)), dma((2, 2 * nz)), dma((2, 2 * nz)),
            dma((2, 4 * nz)), dma((4 * (nz + 2),)), dma((4 * (nz + 2),)),
        ],
        compiler_params=pltpu.CompilerParams(
            collective_id=0, has_side_effects=True, vmem_limit_bytes=60 * 1024 * 1024
        ),
        name="dense_backward",
    )(tokens, grad_out, expert_weights, route_ids, route_prob, device_expert, unit_count)


def shards(tokens, grad_out, route_ids, *rest):
    token_count = tokens.shape[0]
    capacity = token_count * route_ids.shape[1] * 4 // lax.axis_size("expert")
    form = dense_shards if capacity >= token_count else routed_shards
    return form(tokens, grad_out, route_ids, *rest)


def solution(mesh):
    in_specs = (P(AXES, None),) * 4 + (P(), P(), P("expert", None, None))
    out_specs = (P(AXES, None), P("expert", "dp", None))
    return jax.shard_map(shards, mesh=mesh, in_specs=in_specs, out_specs=out_specs, check_vma=False)
```
